32 devices in a mesh: dp: 2 (over core), cent: 16 (over z, y, x).
Axes of the slice: x: 2, y: 2, z: 4, core: 2. Of those that a mesh axis runs over, the one named last changes fastest.
Arguments:
- embeddings: bfloat16 [4096, 768], P(('dp', 'cent')), may hold values from -20 to 20
- fine_centroids: float32 [8192, 768], P('cent'), may hold values from -8 to 8
- parents: int32 [8192], P('cent'), may hold values from 0 to 2047
- coarse_centroids: float32 [2048, 768], P('cent'), may hold values from -6 to 6
Outputs:
- new_fine: float32 [8192, 768], P('cent')
- new_coarse: float32 [2048, 768], P('cent')
The draws below stay inside these ranges and needn't reach their ends.
All inputs are finite; a program needn't handle non-finite values.
Results may differ from the reference program's by a relative error of at most 0.004.
Values may be sent and summed in bfloat16 or wider, within the bound.
A program may use at most 64 MiB of HBM per device.

```python
import math
import jax
import jax.numpy as jnp
from jax import lax

D = 768
KC = 2048
K = 8192
TOTAL = 4096


def centroid_table(key):
    base = jnp.clip(jax.random.normal(jax.random.fold_in(key, 11), (K, D), jnp.float32), -5.0, 5.0)
    return base


def draw_fine_centroids(key, part):
    return centroid_table(key).astype(jnp.float32)


def draw_embeddings(key, part):
    rows = jnp.clip(jax.random.normal(jax.random.fold_in(key, 22), (TOTAL, D), jnp.float32), -6.0, 6.0)
    return rows.astype(jnp.bfloat16)


def plant(array, stream_key, low, top_value):
    place = [jax.random.randint(jax.random.fold_in(stream_key, axis), (), 0, length) for axis, length in enumerate(array.shape)]
    main_axis = array.shape.index(max(array.shape))
    next_to = place[:main_axis] + [(place[main_axis] + 1) % array.shape[main_axis]] + place[main_axis + 1:]
    return array.at[tuple(place)].set(low).at[tuple(next_to)].set(top_value)


def block_levels(key, extent, cuts, smallest, high):
    loudness = 1.0
    for axis_at, shards_of in cuts:
        heights = jax.random.uniform(jax.random.fold_in(jax.random.fold_in(key, 6), axis_at), (shards_of,), jnp.float32, smallest / len(cuts), high / len(cuts))
        loudness = loudness * jnp.repeat(jnp.exp(heights), extent[axis_at] // shards_of).reshape((-1,) + (1,) * (len(extent) - 1 - axis_at))
    return loudness


def normal_values(rng, extent, scale, limit, pieces=(), kind=jnp.bfloat16):
    values = jax.random.normal(rng, extent, jnp.float32) * scale
    if len(pieces) > 0:
        values = block_levels(rng, extent, pieces, -0.22, 0.18) * values
    return jnp.clip(values, min=-limit, max=limit).astype(kind)


def setup_inputs(seed: int = 0) -> dict:
    seeds = jax.random.split(jax.random.key(seed), 5)
    return {
        "embeddings": draw_embeddings(jax.random.fold_in(seeds[4], 71), 0),
        "fine_centroids": draw_fine_centroids(jax.random.fold_in(seeds[4], 71), 0),
        "parents": plant(jax.random.randint(seeds[2], (K,), 0, KC), jax.random.fold_in(seeds[2], 1), 0, KC - 1).astype(jnp.int32),
        "coarse_centroids": normal_values(seeds[3], (KC, D), 1.0, 6.0, ((0, 16),), jnp.float32),
    }


sharpness = 0.1
coarse_prior = 16.0


def reference(embeddings, fine_centroids, parents, coarse_centroids):
    narrow = fine_centroids.astype(jnp.bfloat16)
    half_norm = 0.5 * jnp.sum(fine_centroids * fine_centroids, axis=1)
    row_count = embeddings.shape[0]
    block_rows = math.gcd(row_count, 512)
    row_blocks = embeddings.reshape(row_count // block_rows, block_rows, embeddings.shape[1])

    def sum_step(carried, one_block):
        scores = jnp.dot(one_block, narrow.T, preferred_element_type=jnp.float32)
        logits = sharpness * (scores - half_norm[None, :])
        row_peak = jnp.max(logits, axis=1)
        weights = jnp.exp(logits - row_peak[:, None])
        row_mass = jnp.sum(weights, axis=1)
        soft = weights / row_mass[:, None]
        wide_block = one_block.astype(jnp.float32)
        summed = carried[0] + jnp.dot(soft.T, wide_block, precision=lax.Precision.HIGHEST, preferred_element_type=jnp.float32)
        counted = carried[1] + jnp.sum(soft, axis=0)
        return (summed, counted), None

    start_state = (jnp.zeros(fine_centroids.shape, jnp.float32), jnp.zeros((fine_centroids.shape[0],), jnp.float32))
    (fine_sums, fine_counts), _ = lax.scan(sum_step, start_state, row_blocks)
    pooled = fine_centroids + fine_sums
    mass = 1.0 + fine_counts
    new_fine = pooled / mass[:, None]
    coarse_sum = jax.ops.segment_sum(pooled, parents, num_segments=KC)
    coarse_mass = jax.ops.segment_sum(mass, parents, num_segments=KC)
    new_coarse = (coarse_prior * coarse_centroids + coarse_sum) / (coarse_prior + coarse_mass)[:, None]
    return (new_fine, new_coarse)
```

```python
import functools
import math

import jax
import jax.numpy as jnp
from jax import lax
from jax.experimental import pallas as pl
from jax.experimental.pallas import tpu as pltpu
from jax.sharding import PartitionSpec as P

KC = 2048


sharpness = 0.1
coarse_prior = 16.0


def block_logits(one_block, narrow_centroids, half_norm):
    scores = lax.dot_general(
        one_block, narrow_centroids, (((1,), (1,)), ((), ())), preferred_element_type=jnp.float32
    )
    return sharpness * (scores - half_norm[None, :])


def coarse_terms(parent_ids, pooled, mass_rows):
    summed = jax.ops.segment_sum(pooled, parent_ids, num_segments=KC)
    weighted = jax.ops.segment_sum(mass_rows, parent_ids, num_segments=KC)
    return (summed, weighted)


def local(embeddings, fine_centroids, parents, coarse_centroids):
    gathered = lax.all_gather(embeddings, "cent", axis=0, tiled=True)
    row_count = gathered.shape[0]
    feat_width = gathered.shape[1]
    block_rows = math.gcd(row_count, 512)
    row_blocks = gathered.reshape(row_count // block_rows, block_rows, feat_width)
    narrow_centroids = fine_centroids.astype(jnp.bfloat16)
    half_norm = 0.5 * jnp.sum(fine_centroids * fine_centroids, axis=1)
    no_carry = jnp.zeros((), jnp.float32)

    def peak_step(carried, one_block):
        logits = block_logits(one_block, narrow_centroids, half_norm)
        return (carried, jnp.max(logits, axis=1))

    _, local_peak = lax.scan(peak_step, no_carry, row_blocks)
    row_peak = lax.pmax(local_peak.reshape(-1), "cent")

    def mass_step(carried, items):
        one_block, block_peak = items
        logits = block_logits(one_block, narrow_centroids, half_norm)
        return (carried, jnp.sum(jnp.exp(logits - block_peak[:, None]), axis=1))

    _, local_mass = lax.scan(mass_step, no_carry, (row_blocks, row_peak.reshape(-1, block_rows)))
    row_mass = lax.psum(local_mass.reshape(-1), "cent")

    def sum_step(carried, items):
        one_block, block_peak, block_mass = items
        logits = block_logits(one_block, narrow_centroids, half_norm)
        soft_weights = jnp.exp(logits - block_peak[:, None]) / block_mass[:, None]
        wide_block = one_block.astype(jnp.float32)
        summed = carried[0] + lax.dot_general(
            soft_weights,
            wide_block,
            (((0,), (0,)), ((), ())),
            precision=lax.Precision.HIGHEST,
            preferred_element_type=jnp.float32,
        )
        counted = carried[1] + jnp.sum(soft_weights, axis=0)
        return ((summed, counted), None)

    local_rows = fine_centroids.shape[0]
    start_state = (
        jnp.zeros(fine_centroids.shape, jnp.float32),
        jnp.zeros((local_rows,), jnp.float32),
    )
    stacked = (row_blocks, row_peak.reshape(-1, block_rows), row_mass.reshape(-1, block_rows))
    (fine_sums, fine_counts), _ = lax.scan(sum_step, start_state, stacked)
    total_sums, total_counts = lax.psum((fine_sums, fine_counts), "dp")
    pooled = fine_centroids + total_sums
    mass_rows = 1.0 + total_counts
    new_fine = pooled / mass_rows[:, None]
    col_width = feat_width // lax.axis_size("dp")
    first_col = lax.axis_index("dp") * col_width
    pooled_cols = lax.dynamic_slice_in_dim(pooled, first_col, col_width, 1)
    coarse_sum, coarse_mass = coarse_terms(parents, pooled_cols, mass_rows)
    owned_sum, owned_mass = (
        lax.psum_scatter(coarse_sum, "cent", scatter_dimension=0, tiled=True),
        lax.psum_scatter(coarse_mass, "cent", scatter_dimension=0, tiled=True),
    )
    old_cols = lax.dynamic_slice_in_dim(coarse_centroids, first_col, col_width, 1)
    new_cols = (coarse_prior * old_cols + owned_sum) / (coarse_prior + owned_mass)[:, None]
    new_coarse = lax.all_gather(new_cols, "dp", axis=1, tiled=True)
    return (new_fine, new_coarse)


MESH = pl.DeviceIdType.MESH
NT = (((1,), (1,)), ((), ()))


def dot(a, b):
    return jnp.dot(a, b, preferred_element_type=jnp.float32)


def to_row(col):
    return jnp.transpose(jnp.broadcast_to(col, (col.shape[0], 128)))[0:8]


def to_col(row):
    return jnp.transpose(jnp.broadcast_to(row, (128, row.shape[1])))[:, 0:1]


def step_kernel(
    n, nz, emb, fine, par, coarse, nf, nc,
    G, narrow, pr, wh, wl, st, ss, sr, cs, cr, hi, lo,
    xs, xr, ys, yr, zs, zr, own, ms, mr,
    g_recv, gz_send, gx_send, gy_send, st_send, st_recv,
    sum_send, sum_recv, cnt_sem, nf_send, nf_recv,
    x_send, x_recv, y_send, y_recv, z_send, z_recv, m_sem, nc_sem,
):
    d = lax.axis_index("dp")
    c = lax.axis_index("cent")
    rows = emb.shape[0]
    local, width = fine.shape
    half = width // 2
    coarse_rows = coarse.shape[0]
    x, y, z = c % 2, (c // 2) % 2, c // 4
    xy = c % 4
    nbr_x = c + 1 - 2 * x
    nbr_y = c + 2 - 4 * y
    cols = (xy, xy + 1 - 2 * x, xy + 2 - 4 * y, 3 - xy)
    other = 1 - d

    barrier = pltpu.get_barrier_semaphore()
    for k in range(1, n):
        pl.semaphore_signal(barrier, inc=1, device_id=(d, (c + k) % n), device_id_type=MESH)
    pl.semaphore_signal(barrier, inc=1, device_id=(other, c), device_id_type=MESH)
    pl.semaphore_wait(barrier, n)

    def copy(src, dst, send, recv, core, chip):
        return pltpu.make_async_remote_copy(
            src_ref=src, dst_ref=dst, send_sem=send, recv_sem=recv,
            device_id=(core, chip), device_id_type=MESH,
        )

    def block_copy(src, slot, send, chip):
        return copy(src, G.at[slot], send, g_recv.at[slot], d, chip)

    def arrived(slot):
        copy(G.at[slot], G.at[slot], gz_send.at[0], g_recv.at[slot], d, nbr_x).wait_recv()

    mine = xy * nz + z
    sends = []

    def send_block(src, slot, send, chip):
        one = block_copy(src, slot, send, chip)
        one.start()
        sends.append(one)

    send_block(emb, mine, gx_send.at[0], nbr_x)
    send_block(emb, mine, gy_send.at[0], nbr_y)
    for k in range(1, nz):
        send_block(emb, mine, gz_send.at[k - 1], ((z + k) % nz) * 4 + xy)
    G[mine] = emb[...]
    narrow[...] = fine[...].astype(jnp.bfloat16)
    half_norm = 0.5 * jnp.sum(fine[...] * fine[...], axis=1, keepdims=True)

    def group_logits(r):
        col = cols[r]

        def pair(i, _):
            blocks = G[pl.ds(col * nz + 2 * i, 2)].reshape(2 * rows, width)
            scores = lax.dot_general(narrow[...], blocks, NT, preferred_element_type=jnp.float32)
            logits = sharpness * (scores - half_norm)
            peak = jnp.max(logits, axis=0, keepdims=True)
            weights = jnp.exp(logits - peak)
            mass = jnp.sum(weights, axis=0, keepdims=True)
            pr[r, :, pl.ds(pl.multiple_of(i * (2 * rows), 2 * rows), 2 * rows)] = weights
            for t in range(2):
                st[col, 0, pl.ds(2 * i + t, 1), :] = peak[:, t * rows:(t + 1) * rows]
                st[col, 0, pl.ds(nz + 2 * i + t, 1), :] = mass[:, t * rows:(t + 1) * rows]
            return 0

        lax.fori_loop(0, nz // 2, pair, 0)

    def send_stats(r):
        col = cols[r]
        for k in range(1, n):
            copy(
                st.at[col, 0], st.at[col, n - k], st_send.at[r], st_recv.at[col], d, (c + k) % n
            ).start()

    for k in range(1, nz):
        slot = xy * nz + (z + nz - k) % nz
        arrived(slot)
        send_block(G.at[slot], slot, gx_send.at[k], nbr_x)
        send_block(G.at[slot], slot, gy_send.at[k], nbr_y)
    for k in range(nz // 2):
        slot = cols[1] * nz + (z + nz - k) % nz
        arrived(slot)
        send_block(G.at[slot], slot, gy_send.at[nz + k], nbr_y)
    for k in range(nz // 2, nz):
        slot = cols[2] * nz + (z + nz - k) % nz
        arrived(slot)
        send_block(G.at[slot], slot, gx_send.at[nz + k - nz // 2], nbr_x)
    group_logits(0)
    send_stats(0)
    for k in range(nz // 2, nz):
        arrived(cols[1] * nz + (z + nz - k) % nz)
    group_logits(1)
    send_stats(1)
    for k in range(nz // 2):
        arrived(cols[2] * nz + (z + nz - k) % nz)
    group_logits(2)
    send_stats(2)
    for k in range(nz):
        arrived(cols[3] * nz + (z + nz - k) % nz)
    group_logits(3)
    send_stats(3)

    counts = jnp.zeros((local, 1), jnp.float32)
    for r in range(4):
        col = cols[r]
        pltpu.make_async_copy(
            st.at[col, pl.ds(1, n - 1)], st.at[col, pl.ds(1, n - 1)], st_recv.at[col]
        ).wait()
        peaks = st[col, :, 0:nz, :]
        masses = st[col, :, nz:2 * nz, :]
        top = jnp.max(peaks, axis=0)
        total = jnp.sum(masses * jnp.exp(peaks - top[None]), axis=0)
        factor = jnp.exp(peaks[0] - top) / total
        for t in range(nz):
            lanes = slice(t * rows, (t + 1) * rows)
            soft = pr[r, :, lanes] * factor[t:t + 1, :]
            counts = counts + jnp.sum(soft, axis=1, keepdims=True)
            high = soft.astype(jnp.bfloat16)
            wh[r, :, lanes] = high
            wl[r, :, lanes] = (soft - high.astype(jnp.float32)).astype(jnp.bfloat16)
    cs[...] = to_row(counts)
    count_copy = copy(cs, cr, cnt_sem.at[0], cnt_sem.at[1], other, c)
    count_copy.start()

    own_cols = pl.ds(pl.multiple_of(d * half, 128), half)
    other_cols = pl.ds(pl.multiple_of(other * half, 128), half)
    part = local // 2

    def sums(h, columns):
        picked = pl.ds(h * part, part)
        out = jnp.zeros((part, half), jnp.float32)
        for r in range(4):
            block = G[pl.ds(cols[r] * nz, nz), :, columns].reshape(nz * rows, half)
            out = out + dot(wh[r, picked, :], block) + dot(wl[r, picked, :], block)
        return out

    sum_copies = []
    for h in range(2):
        ss[h] = sums(h, other_cols)
        one = copy(ss.at[h], sr.at[h], sum_send.at[h], sum_recv.at[h], other, c)
        one.start()
        sum_copies.append(one)
    own_sums = [sums(h, own_cols) for h in range(2)]

    count_copy.wait()
    mass_row = 1.0 + (cs[...] + cr[...])
    mass_col = to_col(mass_row[0:1])
    nf_copies = []
    for h in range(2):
        sum_copies[h].wait()
        picked = pl.ds(h * part, part)
        pooled = fine[picked, own_cols] + (own_sums[h] + sr[h])
        high = pooled.astype(jnp.bfloat16)
        hi[picked, :] = high
        lo[picked, :] = (pooled - high.astype(jnp.float32)).astype(jnp.bfloat16)
        nf[picked, own_cols] = pooled / mass_col[h * part:(h + 1) * part]
        one = copy(
            nf.at[picked, own_cols], nf.at[picked, own_cols], nf_send.at[h], nf_recv.at[h], other, c
        )
        one.start()
        nf_copies.append(one)

    one_row = mass_row[0:1]
    first = one_row.astype(jnp.bfloat16).astype(jnp.float32)
    second = (one_row - first).astype(jnp.bfloat16).astype(jnp.float32)
    third = one_row - first - second
    at_row = lax.broadcasted_iota(jnp.int32, (16, local), 0)
    pieces = jnp.where(
        at_row == 0, first, jnp.where(at_row == 1, second, jnp.where(at_row == 2, third, 0.0))
    ).astype(jnp.bfloat16)
    place = lax.broadcasted_iota(jnp.int32, (coarse_rows, local), 0)

    def partial_block(chip):
        hot = (par[...] == place + chip * coarse_rows).astype(jnp.float32).astype(jnp.bfloat16)
        masses = lax.dot_general(pieces, hot, NT, preferred_element_type=jnp.float32)
        ms[chip] = jnp.broadcast_to(jnp.sum(masses, axis=0, keepdims=True), (8, coarse_rows))
        return dot(hot, hi[...]) + dot(hot, lo[...])

    def column_blocks(r, put):
        def one(t, _):
            put(t, partial_block(t * 4 + cols[r]))
            return 0

        lax.fori_loop(0, nz, one, 0)

    low = nz // 2

    def x_copy(i):
        return copy(xs.at[i], xr.at[i], x_send.at[i], x_recv.at[i], d, nbr_x)

    def y_copy(i):
        return copy(ys.at[i], yr.at[i], y_send.at[i], y_recv.at[i], d, nbr_y)

    def put_diag(t, value):
        own[t] = value

    column_blocks(3, put_diag)
    for t in range(low):
        xs[nz + t] = own[t].astype(jnp.bfloat16)
        x_copy(nz + t).start()
        ys[nz + t] = own[low + t].astype(jnp.bfloat16)
        y_copy(nz + t).start()
    column_blocks(1, put_diag)
    for t in range(low):
        xs[t] = own[t].astype(jnp.bfloat16)
        x_copy(t).start()
    for t in range(low):
        y_copy(nz + t).wait_recv()
        xs[low + t] = (own[low + t] + yr[nz + t].astype(jnp.float32)).astype(jnp.bfloat16)
        x_copy(low + t).start()
    column_blocks(2, put_diag)
    for t in range(low):
        ys[low + t] = own[low + t].astype(jnp.bfloat16)
        y_copy(low + t).start()
    for t in range(low):
        x_copy(nz + t).wait_recv()
        ys[t] = (own[t] + xr[nz + t].astype(jnp.float32)).astype(jnp.bfloat16)
        y_copy(t).start()
    column_blocks(0, put_diag)
    for k in range(1, n):
        to = (c + k) % n
        copy(ms.at[to], mr.at[n - k], m_sem.at[0], m_sem.at[1], d, to).start()

    def column_sum(t):
        x_copy(t).wait_recv()
        y_copy(t).wait_recv()
        return own[t] + (xr[t].astype(jnp.float32) + yr[t].astype(jnp.float32))

    z_copies = []
    for k in range(1, nz):
        t = (z + k) % nz
        zs[k - 1] = column_sum(t).astype(jnp.bfloat16)
        one = copy(
            zs.at[k - 1], zr.at[k - 1], z_send.at[k - 1], z_recv.at[k - 1], d, t * 4 + xy
        )
        one.start()
        z_copies.append(one)
    total = column_sum(z)
    pltpu.make_async_copy(mr.at[pl.ds(1, n - 1)], mr.at[pl.ds(1, n - 1)], m_sem.at[1]).wait()
    mass_total = ms[c]
    for k in range(1, n):
        mass_total = mass_total + mr[k]
    mass_total = to_col(mass_total[0:1])
    for k in range(1, nz):
        z_copies[k - 1].wait_recv()
        total = total + zr[k - 1].astype(jnp.float32)
    nc[:, own_cols] = (coarse_prior * coarse[:, own_cols] + total) / (coarse_prior + mass_total)
    last = copy(nc.at[:, own_cols], nc.at[:, own_cols], nc_sem.at[0], nc_sem.at[1], other, c)
    last.start()

    for one in sends + z_copies:
        one.wait_send()
    for r in range(4):
        whole = st.at[cols[r], pl.ds(1, n - 1)]
        pltpu.make_async_copy(whole, whole, st_send.at[r]).wait()
    pltpu.make_async_copy(mr.at[pl.ds(1, n - 1)], mr.at[pl.ds(1, n - 1)], m_sem.at[0]).wait()
    for i in range(nz + low):
        x_copy(i).wait_send()
        y_copy(i).wait_send()
    for one in nf_copies:
        one.wait()
    last.wait()


def fused_step(n, embeddings, fine_centroids, parents, coarse_centroids):
    nz = n // 4
    low = nz // 2
    rows, width = embeddings.shape
    local = fine_centroids.shape[0]
    coarse_rows = coarse_centroids.shape[0]
    half = width // 2
    bf, f32 = jnp.bfloat16, jnp.float32
    vmem = pl.BlockSpec(memory_space=pltpu.VMEM)
    dma = pltpu.SemaphoreType.DMA
    V = pltpu.VMEM
    block = (coarse_rows, half)
    return pl.pallas_call(
        functools.partial(step_kernel, n, nz),
        out_shape=(
            jax.ShapeDtypeStruct(fine_centroids.shape, f32),
            jax.ShapeDtypeStruct(coarse_centroids.shape, f32),
        ),
        in_specs=[vmem] * 4,
        out_specs=(vmem, vmem),
        scratch_shapes=[
            V((n, rows, width), bf),
            V((local, width), bf),
            V((4, local, nz * rows), f32),
            V((4, local, nz * rows), bf),
            V((4, local, nz * rows), bf),
            V((4, n, 2 * nz, rows), f32),
            V((2, local // 2, half), f32),
            V((2, local // 2, half), f32),
            V((8, local), f32),
            V((8, local), f32),
            V((local, half), bf),
            V((local, half), bf),
            V((nz + low,) + block, bf),
            V((nz + low,) + block, bf),
            V((nz + low,) + block, bf),
            V((nz + low,) + block, bf),
            V((nz - 1,) + block, bf),
            V((nz - 1,) + block, bf),
            V((nz,) + block, f32),
            V((n, 8, coarse_rows), f32),
            V((n, 8, coarse_rows), f32),
            dma((n,)), dma((nz - 1,)), dma((nz + low,)), dma((nz + low,)),
            dma((4,)), dma((4,)),
            dma((2,)), dma((2,)), dma((2,)), dma((2,)), dma((2,)),
            dma((nz + low,)), dma((nz + low,)), dma((nz + low,)), dma((nz + low,)),
            dma((nz - 1,)), dma((nz - 1,)), dma((2,)), dma((2,)),
        ],
        compiler_params=pltpu.CompilerParams(collective_id=0, has_side_effects=True),
    )(embeddings, fine_centroids, parents.reshape(1, local), coarse_centroids)


def solution(mesh):
    in_specs = (P(("dp", "cent"), None), P("cent", None), P("cent"), P("cent", None))
    out_specs = (P("cent", None), P("cent", None))
    n, cores = mesh.shape["cent"], mesh.shape["dp"]

    def body(embeddings, fine_centroids, parents, coarse_centroids):
        rows, width = embeddings.shape
        fits = (
            cores == 2
            and n % 8 == 0
            and rows == 128
            and width % 256 == 0
            and fine_centroids.shape[0] % 256 == 0
            and coarse_centroids.shape[0] == 128
        )
        if fits:
            return fused_step(n, embeddings, fine_centroids, parents, coarse_centroids)
        return local(embeddings, fine_centroids, parents, coarse_centroids)

    return jax.shard_map(body, mesh=mesh, in_specs=in_specs, out_specs=out_specs, check_vma=False)
```

```python
import functools
import math

import jax
import jax.numpy as jnp
from jax import lax
from jax.experimental import pallas as pl
from jax.experimental.pallas import tpu as pltpu
from jax.sharding import PartitionSpec as P

KC = 2048


sharpness = 0.1
coarse_prior = 16.0


def block_logits(one_block, narrow_centroids, half_norm):
    scores = lax.dot_general(
        one_block, narrow_centroids, (((1,), (1,)), ((), ())), preferred_element_type=jnp.float32
    )
    return sharpness * (scores - half_norm[None, :])


def coarse_terms(parent_ids, pooled, mass_rows):
    summed = jax.ops.segment_sum(pooled, parent_ids, num_segments=KC)
    weighted = jax.ops.segment_sum(mass_rows, parent_ids, num_segments=KC)
    return (summed, weighted)


def local(embeddings, fine_centroids, parents, coarse_centroids):
    gathered = lax.all_gather(embeddings, "cent", axis=0, tiled=True)
    row_count = gathered.shape[0]
    feat_width = gathered.shape[1]
    block_rows = math.gcd(row_count, 512)
    row_blocks = gathered.reshape(row_count // block_rows, block_rows, feat_width)
    narrow_centroids = fine_centroids.astype(jnp.bfloat16)
    half_norm = 0.5 * jnp.sum(fine_centroids * fine_centroids, axis=1)
    no_carry = jnp.zeros((), jnp.float32)

    def peak_step(carried, one_block):
        logits = block_logits(one_block, narrow_centroids, half_norm)
        return (carried, jnp.max(logits, axis=1))

    _, local_peak = lax.scan(peak_step, no_carry, row_blocks)
    row_peak = lax.pmax(local_peak.reshape(-1), "cent")

    def mass_step(carried, items):
        one_block, block_peak = items
        logits = block_logits(one_block, narrow_centroids, half_norm)
        return (carried, jnp.sum(jnp.exp(logits - block_peak[:, None]), axis=1))

    _, local_mass = lax.scan(mass_step, no_carry, (row_blocks, row_peak.reshape(-1, block_rows)))
    row_mass = lax.psum(local_mass.reshape(-1), "cent")

    def sum_step(carried, items):
        one_block, block_peak, block_mass = items
        logits = block_logits(one_block, narrow_centroids, half_norm)
        soft_weights = jnp.exp(logits - block_peak[:, None]) / block_mass[:, None]
        wide_block = one_block.astype(jnp.float32)
        summed = carried[0] + lax.dot_general(
            soft_weights,
            wide_block,
            (((0,), (0,)), ((), ())),
            precision=lax.Precision.HIGHEST,
            preferred_element_type=jnp.float32,
        )
        counted = carried[1] + jnp.sum(soft_weights, axis=0)
        return ((summed, counted), None)

    local_rows = fine_centroids.shape[0]
    start_state = (
        jnp.zeros(fine_centroids.shape, jnp.float32),
        jnp.zeros((local_rows,), jnp.float32),
    )
    stacked = (row_blocks, row_peak.reshape(-1, block_rows), row_mass.reshape(-1, block_rows))
    (fine_sums, fine_counts), _ = lax.scan(sum_step, start_state, stacked)
    total_sums, total_counts = lax.psum((fine_sums, fine_counts), "dp")
    pooled = fine_centroids + total_sums
    mass_rows = 1.0 + total_counts
    new_fine = pooled / mass_rows[:, None]
    col_width = feat_width // lax.axis_size("dp")
    first_col = lax.axis_index("dp") * col_width
    pooled_cols = lax.dynamic_slice_in_dim(pooled, first_col, col_width, 1)
    coarse_sum, coarse_mass = coarse_terms(parents, pooled_cols, mass_rows)
    owned_sum, owned_mass = (
        lax.psum_scatter(coarse_sum, "cent", scatter_dimension=0, tiled=True),
        lax.psum_scatter(coarse_mass, "cent", scatter_dimension=0, tiled=True),
    )
    old_cols = lax.dynamic_slice_in_dim(coarse_centroids, first_col, col_width, 1)
    new_cols = (coarse_prior * old_cols + owned_sum) / (coarse_prior + owned_mass)[:, None]
    new_coarse = lax.all_gather(new_cols, "dp", axis=1, tiled=True)
    return (new_fine, new_coarse)


MESH = pl.DeviceIdType.MESH
NT = (((1,), (1,)), ((), ()))


def dot(a, b):
    return jnp.dot(a, b, preferred_element_type=jnp.float32)


def to_row(col):
    return jnp.transpose(jnp.broadcast_to(col, (col.shape[0], 128)))[0:8]


def to_col(row):
    return jnp.transpose(jnp.broadcast_to(row, (128, row.shape[1])))[:, 0:1]


def step_kernel(
    n, nz, emb, fine, par, coarse, nf, nc,
    G, narrow, pr, wh, wl, st, ss, sr, cs, cr, hi, lo,
    xs, xr, ys, yr, zs, zr, own, ms, mr,
    g_recv, gz_send, gx_send, gy_send, st_send, st_recv,
    sum_send, sum_recv, cnt_sem, nf_send, nf_recv,
    x_send, x_recv, y_send, y_recv, z_send, z_recv, m_sem, nc_sem,
):
    d = lax.axis_index("dp")
    c = lax.axis_index("cent")
    rows = emb.shape[0]
    local, width = fine.shape
    half = width // 2
    coarse_rows = coarse.shape[0]
    x, y, z = c % 2, (c // 2) % 2, c // 4
    xy = c % 4
    nbr_x = c + 1 - 2 * x
    nbr_y = c + 2 - 4 * y
    cols = (xy, xy + 1 - 2 * x, xy + 2 - 4 * y, 3 - xy)
    other = 1 - d

    barrier = pltpu.get_barrier_semaphore()
    for k in range(1, n):
        pl.semaphore_signal(barrier, inc=1, device_id=(d, (c + k) % n), device_id_type=MESH)
    pl.semaphore_signal(barrier, inc=1, device_id=(other, c), device_id_type=MESH)
    pl.semaphore_wait(barrier, n)

    def copy(src, dst, send, recv, core, chip):
        return pltpu.make_async_remote_copy(
            src_ref=src, dst_ref=dst, send_sem=send, recv_sem=recv,
            device_id=(core, chip), device_id_type=MESH,
        )

    def near(i):
        mirror = z >= nz // 2
        at = jnp.where(mirror, nz - 1 - z, z)
        step = (i + 1) // 2
        found = jnp.where(i <= 2 * at, at - step if i % 2 else at + step, i)
        return jnp.where(mirror, nz - 1 - found, found)

    order = [near(i) for i in range(nz)]
    low = nz // 2

    piece = rows // 2

    def piece_of(slot, h):
        return G.at[slot, pl.ds(h * piece, piece)]

    def piece_copy(src, slot, h, send, chip):
        return copy(src, piece_of(slot, h), send, g_recv.at[slot * 2 + h], d, chip)

    def arrived(slot, h):
        piece_copy(piece_of(slot, h), slot, h, gx_send.at[0], nbr_x).wait_recv()

    sends = []
    maybe_sends = []

    def send_piece(src, slot, h, send, chip):
        one = piece_copy(src, slot, h, send, chip)
        one.start()
        sends.append(one)

    def send_along(src, slot, h, send, to_z):
        exists = jnp.logical_and(to_z >= 0, to_z < nz)
        one = piece_copy(src, slot, h, send, to_z * 4 + xy)

        @pl.when(exists)
        def _():
            one.start()

        maybe_sends.append((exists, one))

    mine = xy * nz + z
    for h in range(2):
        src = emb.at[pl.ds(h * piece, piece)]
        send_along(src, mine, h, gz_send.at[h], z + 1)
        send_along(src, mine, h, gz_send.at[2 + h], z - 1)
        send_piece(src, mine, h, gx_send.at[h], nbr_x)
        send_piece(src, mine, h, gy_send.at[h], nbr_y)
    G[mine] = emb[...]
    narrow[...] = fine[...].astype(jnp.bfloat16)
    half_norm = 0.5 * jnp.sum(fine[...] * fine[...], axis=1, keepdims=True)

    def block_logits(r, i):
        col, o = cols[r], order[i]
        scores = lax.dot_general(
            narrow[...], G[col * nz + o], NT, preferred_element_type=jnp.float32
        )
        logits = sharpness * (scores - half_norm)
        peak = jnp.max(logits, axis=0, keepdims=True)
        weights = jnp.exp(logits - peak)
        pr[r, :, pl.ds(pl.multiple_of(o * rows, rows), rows)] = weights
        st[col, 0, pl.ds(o, 1), :] = peak
        st[col, 0, pl.ds(nz + o, 1), :] = jnp.sum(weights, axis=0, keepdims=True)

    def send_stats(r):
        col = cols[r]
        for k in range(1, n):
            copy(
                st.at[col, 0], st.at[col, n - k], st_send.at[r], st_recv.at[col], d, (c + k) % n
            ).start()

    def forward_column(i):
        o = order[i]
        slot = xy * nz + o
        to_z = jnp.where(o < z, z + 1, z - 1)
        for h in range(2):
            arrived(slot, h)
            block = piece_of(slot, h)
            send_along(block, slot, h, gz_send.at[2 * i + 2 + h], to_z)
            send_piece(block, slot, h, gx_send.at[2 * i + h], nbr_x)
            send_piece(block, slot, h, gy_send.at[2 * i + h], nbr_y)

    def forward_sides(i):
        o = order[i]
        for h in range(2):
            for r in (1, 2):
                arrived(cols[r] * nz + o, h)
            if i < low:
                slot = cols[1] * nz + o
                send_piece(piece_of(slot, h), slot, h, gy_send.at[2 * (nz + i) + h], nbr_y)
            else:
                slot = cols[2] * nz + o
                send_piece(piece_of(slot, h), slot, h, gx_send.at[2 * (nz + i - low) + h], nbr_x)

    block_logits(0, 0)
    for i in range(1, nz):
        forward_column(i)
        forward_sides(i - 1)
        block_logits(0, i)
        block_logits(1, i - 1)
        block_logits(2, i - 1)
    send_stats(0)
    forward_sides(nz - 1)
    for r in (1, 2):
        block_logits(r, nz - 1)
        send_stats(r)
    for i in range(nz):
        for h in range(2):
            arrived(cols[3] * nz + order[i], h)
        block_logits(3, i)
    send_stats(3)

    counts = jnp.zeros((local, 1), jnp.float32)
    for r in range(4):
        col = cols[r]
        pltpu.make_async_copy(
            st.at[col, pl.ds(1, n - 1)], st.at[col, pl.ds(1, n - 1)], st_recv.at[col]
        ).wait()
        peaks = st[col, :, 0:nz, :]
        masses = st[col, :, nz:2 * nz, :]
        top = jnp.max(peaks, axis=0)
        total = jnp.sum(masses * jnp.exp(peaks - top[None]), axis=0)
        factor = jnp.exp(peaks[0] - top) / total
        for t in range(nz):
            lanes = slice(t * rows, (t + 1) * rows)
            soft = pr[r, :, lanes] * factor[t:t + 1, :]
            counts = counts + jnp.sum(soft, axis=1, keepdims=True)
            high = soft.astype(jnp.bfloat16)
            wh[r, :, lanes] = high
            wl[r, :, lanes] = (soft - high.astype(jnp.float32)).astype(jnp.bfloat16)
    cs[...] = to_row(counts)
    count_copy = copy(cs, cr, cnt_sem.at[0], cnt_sem.at[1], other, c)
    count_copy.start()

    own_cols = pl.ds(pl.multiple_of(d * half, 128), half)
    other_cols = pl.ds(pl.multiple_of(other * half, 128), half)
    part = local // 2

    def sums(h, columns):
        picked = pl.ds(h * part, part)
        out = jnp.zeros((part, half), jnp.float32)
        for r in range(4):
            block = G[pl.ds(cols[r] * nz, nz), :, columns].reshape(nz * rows, half)
            out = out + dot(wh[r, picked, :], block) + dot(wl[r, picked, :], block)
        return out

    sum_copies = []
    for h in range(2):
        ss[h] = sums(h, other_cols)
        one = copy(ss.at[h], sr.at[h], sum_send.at[h], sum_recv.at[h], other, c)
        one.start()
        sum_copies.append(one)
    own_sums = [sums(h, own_cols) for h in range(2)]

    count_copy.wait()
    mass_row = 1.0 + (cs[...] + cr[...])
    mass_col = to_col(mass_row[0:1])
    nf_copies = []
    for h in range(2):
        sum_copies[h].wait()
        picked = pl.ds(h * part, part)
        pooled = fine[picked, own_cols] + (own_sums[h] + sr[h])
        high = pooled.astype(jnp.bfloat16)
        hi[picked, :] = high
        lo[picked, :] = (pooled - high.astype(jnp.float32)).astype(jnp.bfloat16)
        nf[picked, own_cols] = pooled / mass_col[h * part:(h + 1) * part]
        one = copy(
            nf.at[picked, own_cols], nf.at[picked, own_cols], nf_send.at[h], nf_recv.at[h], other, c
        )
        one.start()
        nf_copies.append(one)

    one_row = mass_row[0:1]
    first = one_row.astype(jnp.bfloat16).astype(jnp.float32)
    second = (one_row - first).astype(jnp.bfloat16).astype(jnp.float32)
    third = one_row - first - second
    at_row = lax.broadcasted_iota(jnp.int32, (16, local), 0)
    pieces = jnp.where(
        at_row == 0, first, jnp.where(at_row == 1, second, jnp.where(at_row == 2, third, 0.0))
    ).astype(jnp.bfloat16)
    place = lax.broadcasted_iota(jnp.int32, (coarse_rows, local), 0)

    def partial_block(chip):
        hot = (par[...] == place + chip * coarse_rows).astype(jnp.float32).astype(jnp.bfloat16)
        masses = lax.dot_general(pieces, hot, NT, preferred_element_type=jnp.float32)
        ms[chip] = jnp.broadcast_to(jnp.sum(masses, axis=0, keepdims=True), (8, coarse_rows))
        return dot(hot, hi[...]) + dot(hot, lo[...])

    def x_copy(i):
        return copy(xs.at[i], xr.at[i], x_send.at[i], x_recv.at[i], d, nbr_x)

    def y_copy(i):
        return copy(ys.at[i], yr.at[i], y_send.at[i], y_recv.at[i], d, nbr_y)

    def partial(r, i):
        return partial_block(order[i] * 4 + cols[r])

    def send_x(i, value):
        xs[i] = value.astype(jnp.bfloat16)
        x_copy(i).start()

    def send_y(i, value):
        ys[i] = value.astype(jnp.bfloat16)
        y_copy(i).start()

    for t in range(low):
        send_x(nz + t, partial(3, nz - 1 - t))
        send_y(nz + t, partial(3, low - 1 - t))
    for t in range(low):
        i = nz - 1 - t
        send_x(i, partial(1, i))
        far = partial(2, i)
        x_copy(nz + t).wait_recv()
        send_y(i, far + xr[nz + t].astype(jnp.float32))
    for t in range(low):
        i = low - 1 - t
        send_y(i, partial(2, i))
        close = partial(1, i)
        y_copy(nz + t).wait_recv()
        send_x(i, close + yr[nz + t].astype(jnp.float32))
    for i in range(nz):
        own[i] = partial(0, i)
    for k in range(1, n):
        to = (c + k) % n
        copy(ms.at[to], mr.at[n - k], m_sem.at[0], m_sem.at[1], d, to).start()

    def column_sum(i):
        x_copy(i).wait_recv()
        y_copy(i).wait_recv()
        return own[i] + (xr[i].astype(jnp.float32) + yr[i].astype(jnp.float32))

    def z_copy(i):
        to_z = order[i]
        return copy(
            zs.at[i], zr.at[z], z_send.at[i], z_recv.at[z], d, to_z * 4 + xy
        )

    for i in range(nz - 1, 0, -1):
        zs[i] = column_sum(i).astype(jnp.bfloat16)
        z_copy(i).start()
    total = column_sum(0)
    pltpu.make_async_copy(mr.at[pl.ds(1, n - 1)], mr.at[pl.ds(1, n - 1)], m_sem.at[1]).wait()
    mass_total = ms[c]
    for k in range(1, n):
        mass_total = mass_total + mr[k]
    mass_total = to_col(mass_total[0:1])
    for i in range(nz - 1, 0, -1):
        o = order[i]
        copy(zs.at[i], zr.at[o], z_send.at[i], z_recv.at[o], d, o * 4 + xy).wait_recv()
        total = total + zr[o].astype(jnp.float32)
    nc[:, own_cols] = (coarse_prior * coarse[:, own_cols] + total) / (coarse_prior + mass_total)
    last = copy(nc.at[:, own_cols], nc.at[:, own_cols], nc_sem.at[0], nc_sem.at[1], other, c)
    last.start()

    for one in sends:
        one.wait_send()
    for exists, one in maybe_sends:
        @pl.when(exists)
        def _(one=one):
            one.wait_send()

    for i in range(1, nz):
        z_copy(i).wait_send()
    for r in range(4):
        whole = st.at[cols[r], pl.ds(1, n - 1)]
        pltpu.make_async_copy(whole, whole, st_send.at[r]).wait()
    pltpu.make_async_copy(mr.at[pl.ds(1, n - 1)], mr.at[pl.ds(1, n - 1)], m_sem.at[0]).wait()
    for i in range(nz + low):
        x_copy(i).wait_send()
        y_copy(i).wait_send()
    for one in nf_copies:
        one.wait()
    last.wait()


def fused_step(n, embeddings, fine_centroids, parents, coarse_centroids):
    nz = n // 4
    low = nz // 2
    rows, width = embeddings.shape
    local = fine_centroids.shape[0]
    coarse_rows = coarse_centroids.shape[0]
    half = width // 2
    bf, f32 = jnp.bfloat16, jnp.float32
    vmem = pl.BlockSpec(memory_space=pltpu.VMEM)
    dma = pltpu.SemaphoreType.DMA
    V = pltpu.VMEM
    block = (coarse_rows, half)
    return pl.pallas_call(
        functools.partial(step_kernel, n, nz),
        out_shape=(
            jax.ShapeDtypeStruct(fine_centroids.shape, f32),
            jax.ShapeDtypeStruct(coarse_centroids.shape, f32),
        ),
        in_specs=[vmem] * 4,
        out_specs=(vmem, vmem),
        scratch_shapes=[
            V((n, rows, width), bf),
            V((local, width), bf),
            V((4, local, nz * rows), f32),
            V((4, local, nz * rows), bf),
            V((4, local, nz * rows), bf),
            V((4, n, 2 * nz, rows), f32),
            V((2, local // 2, half), f32),
            V((2, local // 2, half), f32),
            V((8, local), f32),
            V((8, local), f32),
            V((local, half), bf),
            V((local, half), bf),
            V((nz + low,) + block, bf),
            V((nz + low,) + block, bf),
            V((nz + low,) + block, bf),
            V((nz + low,) + block, bf),
            V((nz,) + block, bf),
            V((nz,) + block, bf),
            V((nz,) + block, f32),
            V((n, 8, coarse_rows), f32),
            V((n, 8, coarse_rows), f32),
            dma((2 * n,)), dma((2 * nz + 2,)), dma((2 * (nz + low),)), dma((2 * (nz + low),)),
            dma((4,)), dma((4,)),
            dma((2,)), dma((2,)), dma((2,)), dma((2,)), dma((2,)),
            dma((nz + low,)), dma((nz + low,)), dma((nz + low,)), dma((nz + low,)),
            dma((nz,)), dma((nz,)), dma((2,)), dma((2,)),
        ],
        compiler_params=pltpu.CompilerParams(collective_id=0, has_side_effects=True),
    )(embeddings, fine_centroids, parents.reshape(1, local), coarse_centroids)


def solution(mesh):
    in_specs = (P(("dp", "cent"), None), P("cent", None), P("cent"), P("cent", None))
    out_specs = (P("cent", None), P("cent", None))
    n, cores = mesh.shape["cent"], mesh.shape["dp"]

    def body(embeddings, fine_centroids, parents, coarse_centroids):
        rows, width = embeddings.shape
        fits = (
            cores == 2
            and n % 8 == 0
            and rows == 128
            and width % 256 == 0
            and fine_centroids.shape[0] % 256 == 0
            and coarse_centroids.shape[0] == 128
        )
        if fits:
            return fused_step(n, embeddings, fine_centroids, parents, coarse_centroids)
        return local(embeddings, fine_centroids, parents, coarse_centroids)

    return jax.shard_map(body, mesh=mesh, in_specs=in_specs, out_specs=out_specs, check_vma=False)
```

```python
import functools
import math

import jax
import jax.numpy as jnp
from jax import lax
from jax.experimental import pallas as pl
from jax.experimental.pallas import tpu as pltpu
from jax.sharding import PartitionSpec as P

KC = 2048


sharpness = 0.1
coarse_prior = 16.0


def block_logits(one_block, narrow_centroids, half_norm):
    scores = lax.dot_general(
        one_block, narrow_centroids, (((1,), (1,)), ((), ())), preferred_element_type=jnp.float32
    )
    return sharpness * (scores - half_norm[None, :])


def coarse_terms(parent_ids, pooled, mass_rows):
    summed = jax.ops.segment_sum(pooled, parent_ids, num_segments=KC)
    weighted = jax.ops.segment_sum(mass_rows, parent_ids, num_segments=KC)
    return (summed, weighted)


def local(embeddings, fine_centroids, parents, coarse_centroids):
    gathered = lax.all_gather(embeddings, "cent", axis=0, tiled=True)
    row_count = gathered.shape[0]
    feat_width = gathered.shape[1]
    block_rows = math.gcd(row_count, 512)
    row_blocks = gathered.reshape(row_count // block_rows, block_rows, feat_width)
    narrow_centroids = fine_centroids.astype(jnp.bfloat16)
    half_norm = 0.5 * jnp.sum(fine_centroids * fine_centroids, axis=1)
    no_carry = jnp.zeros((), jnp.float32)

    def peak_step(carried, one_block):
        logits = block_logits(one_block, narrow_centroids, half_norm)
        return (carried, jnp.max(logits, axis=1))

    _, local_peak = lax.scan(peak_step, no_carry, row_blocks)
    row_peak = lax.pmax(local_peak.reshape(-1), "cent")

    def mass_step(carried, items):
        one_block, block_peak = items
        logits = block_logits(one_block, narrow_centroids, half_norm)
        return (carried, jnp.sum(jnp.exp(logits - block_peak[:, None]), axis=1))

    _, local_mass = lax.scan(mass_step, no_carry, (row_blocks, row_peak.reshape(-1, block_rows)))
    row_mass = lax.psum(local_mass.reshape(-1), "cent")

    def sum_step(carried, items):
        one_block, block_peak, block_mass = items
        logits = block_logits(one_block, narrow_centroids, half_norm)
        soft_weights = jnp.exp(logits - block_peak[:, None]) / block_mass[:, None]
        wide_block = one_block.astype(jnp.float32)
        summed = carried[0] + lax.dot_general(
            soft_weights,
            wide_block,
            (((0,), (0,)), ((), ())),
            precision=lax.Precision.HIGHEST,
            preferred_element_type=jnp.float32,
        )
        counted = carried[1] + jnp.sum(soft_weights, axis=0)
        return ((summed, counted), None)

    local_rows = fine_centroids.shape[0]
    start_state = (
        jnp.zeros(fine_centroids.shape, jnp.float32),
        jnp.zeros((local_rows,), jnp.float32),
    )
    stacked = (row_blocks, row_peak.reshape(-1, block_rows), row_mass.reshape(-1, block_rows))
    (fine_sums, fine_counts), _ = lax.scan(sum_step, start_state, stacked)
    total_sums, total_counts = lax.psum((fine_sums, fine_counts), "dp")
    pooled = fine_centroids + total_sums
    mass_rows = 1.0 + total_counts
    new_fine = pooled / mass_rows[:, None]
    col_width = feat_width // lax.axis_size("dp")
    first_col = lax.axis_index("dp") * col_width
    pooled_cols = lax.dynamic_slice_in_dim(pooled, first_col, col_width, 1)
    coarse_sum, coarse_mass = coarse_terms(parents, pooled_cols, mass_rows)
    owned_sum, owned_mass = (
        lax.psum_scatter(coarse_sum, "cent", scatter_dimension=0, tiled=True),
        lax.psum_scatter(coarse_mass, "cent", scatter_dimension=0, tiled=True),
    )
    old_cols = lax.dynamic_slice_in_dim(coarse_centroids, first_col, col_width, 1)
    new_cols = (coarse_prior * old_cols + owned_sum) / (coarse_prior + owned_mass)[:, None]
    new_coarse = lax.all_gather(new_cols, "dp", axis=1, tiled=True)
    return (new_fine, new_coarse)


MESH = pl.DeviceIdType.MESH
NT = (((1,), (1,)), ((), ()))


def dot(a, b):
    return jnp.dot(a, b, preferred_element_type=jnp.float32)


def to_row(col):
    return jnp.transpose(jnp.broadcast_to(col, (col.shape[0], 128)))[0:8]


def to_col(row):
    return jnp.transpose(jnp.broadcast_to(row, (128, row.shape[1])))[:, 0:1]


def step_kernel(
    n, nz, emb, fine_hbm, par, coarse, nf_hbm, nc,
    fine, nf, acc,
    G, narrow, pr, wh, st, ss, sr, cs, cr, hi, lo,
    xs, xr, ys, yr, zs, zr, own, ms, mr,
    g_recv, gz_send, gx_send, gy_send, st_send, st_recv,
    sum_send, sum_recv, cnt_sem, nf_send, nf_recv,
    x_send, x_recv, y_send, y_recv, z_send, z_recv, m_sem, nc_sem, load_sem, store_sem,
):
    d = lax.axis_index("dp")
    c = lax.axis_index("cent")
    rows = emb.shape[0]
    local, width = fine.shape
    half = width // 2
    coarse_rows = coarse.shape[0]
    x, y, z = c % 2, (c // 2) % 2, c // 4
    xy = c % 4
    nbr_x = c + 1 - 2 * x
    nbr_y = c + 2 - 4 * y
    cols = (xy, xy + 1 - 2 * x, xy + 2 - 4 * y, 3 - xy)
    other = 1 - d

    barrier = pltpu.get_barrier_semaphore()

    def greet(core, chip):
        pl.semaphore_signal(barrier, inc=1, device_id=(core, chip), device_id_type=MESH)

    fine_in = pltpu.make_async_copy(fine_hbm, fine, load_sem.at[0])
    emb_in = pltpu.make_async_copy(emb, G.at[xy * nz + z], load_sem.at[1])
    greet(d, nbr_x)
    greet(d, nbr_y)
    greet(other, c)

    @pl.when(z > 0)
    def _():
        greet(d, c - 4)

    @pl.when(z < nz - 1)
    def _():
        greet(d, c + 4)

    fine_in.start()
    emb_in.start()
    pl.semaphore_wait(barrier, 3 + jnp.where(z > 0, 1, 0) + jnp.where(z < nz - 1, 1, 0))

    def copy(src, dst, send, recv, core, chip):
        return pltpu.make_async_remote_copy(
            src_ref=src, dst_ref=dst, send_sem=send, recv_sem=recv,
            device_id=(core, chip), device_id_type=MESH,
        )

    def near(i):
        mirror = z >= nz // 2
        at = jnp.where(mirror, nz - 1 - z, z)
        step = (i + 1) // 2
        found = jnp.where(i <= 2 * at, at - step if i % 2 else at + step, i)
        return jnp.where(mirror, nz - 1 - found, found)

    order = [near(i) for i in range(nz)]
    low = nz // 2

    piece = rows // 2

    def piece_of(slot, h):
        return G.at[slot, pl.ds(h * piece, piece)]

    def piece_copy(src, slot, h, send, chip):
        return copy(src, piece_of(slot, h), send, g_recv.at[slot * 2 + h], d, chip)

    def arrived(slot, h):
        piece_copy(piece_of(slot, h), slot, h, gx_send.at[0], nbr_x).wait_recv()

    sends = []
    maybe_sends = []

    def send_piece(src, slot, h, send, chip):
        one = piece_copy(src, slot, h, send, chip)
        one.start()
        sends.append(one)

    def send_along(src, slot, h, send, to_z):
        exists = jnp.logical_and(to_z >= 0, to_z < nz)
        one = piece_copy(src, slot, h, send, to_z * 4 + xy)

        @pl.when(exists)
        def _():
            one.start()

        maybe_sends.append((exists, one))

    mine = xy * nz + z
    for h in range(2):
        src = emb.at[pl.ds(h * piece, piece)]
        send_along(src, mine, h, gz_send.at[h], z + 1)
        send_along(src, mine, h, gz_send.at[2 + h], z - 1)
        send_piece(src, mine, h, gx_send.at[h], nbr_x)
        send_piece(src, mine, h, gy_send.at[h], nbr_y)
    fine_in.wait()
    narrow[...] = fine[...].astype(jnp.bfloat16)
    half_norm = 0.5 * jnp.sum(fine[...] * fine[...], axis=1, keepdims=True)

    def block_logits(r, i):
        col, o = cols[r], order[i]
        scores = lax.dot_general(
            narrow[...], G[col * nz + o], NT, preferred_element_type=jnp.float32
        )
        logits = sharpness * (scores - half_norm)
        peak = jnp.max(logits, axis=0, keepdims=True)
        weights = jnp.exp(logits - peak)
        pr[r, :, pl.ds(pl.multiple_of(o * rows, rows), rows)] = weights
        st[col, 0, pl.ds(o, 1), :] = peak
        st[col, 0, pl.ds(nz + o, 1), :] = jnp.sum(weights, axis=0, keepdims=True)

    def send_stats(r):
        col = cols[r]
        for k in range(1, n):
            copy(
                st.at[col, 0], st.at[col, n - k], st_send.at[r], st_recv.at[col], d, (c + k) % n
            ).start()

    def forward_column(i):
        o = order[i]
        slot = xy * nz + o
        to_z = jnp.where(o < z, z + 1, z - 1)
        for h in range(2):
            arrived(slot, h)
            block = piece_of(slot, h)
            send_along(block, slot, h, gz_send.at[2 * i + 2 + h], to_z)
            send_piece(block, slot, h, gx_send.at[2 * i + h], nbr_x)
            send_piece(block, slot, h, gy_send.at[2 * i + h], nbr_y)

    def relay_y(i):
        slot = cols[1] * nz + order[i]
        for h in range(2):
            send_piece(piece_of(slot, h), slot, h, gy_send.at[2 * (nz + i) + h], nbr_y)

    def forward_sides(i):
        o = order[i]
        for h in range(2):
            for r in (2, 1):
                slot = cols[r] * nz + o
                arrived(slot, h)
                if r == 2 and i >= low:
                    send = gx_send.at[2 * (nz + i - low) + h]
                    send_piece(piece_of(slot, h), slot, h, send, nbr_x)

    emb_in.wait()
    block_logits(0, 0)
    for i in range(1, nz):
        forward_column(i)
        if i == nz - 1:
            for t in range(low):
                relay_y(t)
        forward_sides(i - 1)
        block_logits(0, i)
        block_logits(1, i - 1)
        block_logits(2, i - 1)
    forward_sides(nz - 1)
    send_stats(0)
    for r in (1, 2):
        block_logits(r, nz - 1)
        send_stats(r)
    for i in range(nz):
        for h in range(2):
            arrived(cols[3] * nz + order[i], h)
        block_logits(3, i)
    send_stats(3)

    def column_weights(r, counts):
        col = cols[r]
        pltpu.make_async_copy(
            st.at[col, pl.ds(1, n - 1)], st.at[col, pl.ds(1, n - 1)], st_recv.at[col]
        ).wait()
        peaks = st[col, :, 0:nz, :]
        masses = st[col, :, nz:2 * nz, :]
        top = jnp.max(peaks, axis=0)
        total = jnp.sum(masses * jnp.exp(peaks - top[None]), axis=0)
        factor = jnp.exp(peaks[0] - top) / total
        for t in range(nz):
            lanes = slice(t * rows, (t + 1) * rows)
            soft = (pr[r, :, lanes] * factor[t:t + 1, :]).astype(jnp.bfloat16)
            wh[r, :, lanes] = soft
            counts = counts + soft.astype(jnp.float32)
        return counts

    own_cols = pl.ds(pl.multiple_of(d * half, 128), half)
    other_cols = pl.ds(pl.multiple_of(other * half, 128), half)
    part = local // 2

    def column_sums(r, h, columns):
        block = G[pl.ds(cols[r] * nz, nz), :, columns].reshape(nz * rows, half)
        return dot(wh[r, pl.ds(h * part, part), :], block)

    spread = jnp.zeros((local, rows), jnp.float32)
    for r in range(3):
        spread = column_weights(r, spread)
    for side, columns in enumerate((other_cols, own_cols)):
        for h in range(2):
            acc[side, h] = (
                column_sums(0, h, columns) + column_sums(1, h, columns)
            ) + column_sums(2, h, columns)
    spread = column_weights(3, spread)
    sum_copies = []
    for h in range(2):
        ss[h] = acc[0, h] + column_sums(3, h, other_cols)
        one = copy(ss.at[h], sr.at[h], sum_send.at[h], sum_recv.at[h], other, c)
        one.start()
        sum_copies.append(one)
    cs[...] = to_row(jnp.sum(spread, axis=1, keepdims=True))
    count_copy = copy(cs, cr, cnt_sem.at[0], cnt_sem.at[1], other, c)
    count_copy.start()
    own_sums = [acc[1, h] + column_sums(3, h, own_cols) for h in range(2)]

    count_copy.wait()
    mass_row = 1.0 + (cs[...] + cr[...])
    mass_col = to_col(mass_row[0:1])
    nf_copies = []
    for h in range(2):
        sum_copies[h].wait()
        picked = pl.ds(h * part, part)
        pooled = fine[picked, own_cols] + (own_sums[h] + sr[h])
        high = pooled.astype(jnp.bfloat16)
        hi[picked, :] = high
        lo[picked, :] = (pooled - high.astype(jnp.float32)).astype(jnp.bfloat16)
        nf[picked, own_cols] = pooled / mass_col[h * part:(h + 1) * part]
        one = copy(
            nf.at[picked, own_cols], nf.at[picked, own_cols], nf_send.at[h], nf_recv.at[h], other, c
        )
        one.start()
        nf_copies.append(one)

    one_row = mass_row[0:1]
    first = one_row.astype(jnp.bfloat16).astype(jnp.float32)
    second = (one_row - first).astype(jnp.bfloat16).astype(jnp.float32)
    third = one_row - first - second
    at_row = lax.broadcasted_iota(jnp.int32, (16, local), 0)
    pieces = jnp.where(
        at_row == 0, first, jnp.where(at_row == 1, second, jnp.where(at_row == 2, third, 0.0))
    ).astype(jnp.bfloat16)
    place = lax.broadcasted_iota(jnp.int32, (coarse_rows, local), 0)

    def partial_block(chip):
        hot = (par[...] == place + chip * coarse_rows).astype(jnp.float32).astype(jnp.bfloat16)
        masses = lax.dot_general(pieces, hot, NT, preferred_element_type=jnp.float32)
        ms[chip] = jnp.broadcast_to(jnp.sum(masses, axis=0, keepdims=True), (8, coarse_rows))
        return dot(hot, hi[...]) + dot(hot, lo[...])

    def x_copy(i):
        return copy(xs.at[i], xr.at[i], x_send.at[i], x_recv.at[i], d, nbr_x)

    def y_copy(i):
        return copy(ys.at[i], yr.at[i], y_send.at[i], y_recv.at[i], d, nbr_y)

    def partial(r, i):
        return partial_block(order[i] * 4 + cols[r])

    def send_x(i, value):
        xs[i] = value.astype(jnp.bfloat16)
        x_copy(i).start()

    def send_y(i, value):
        ys[i] = value.astype(jnp.bfloat16)
        y_copy(i).start()

    for t in range(low):
        send_x(nz + t, partial(3, nz - 1 - t))
        send_y(nz + t, partial(3, low - 1 - t))
    for t in range(low):
        i = nz - 1 - t
        send_x(i, partial(1, i))
        far = partial(2, i)
        x_copy(nz + t).wait_recv()
        send_y(i, far + xr[nz + t].astype(jnp.float32))
    for t in range(low):
        i = low - 1 - t
        send_y(i, partial(2, i))
        close = partial(1, i)
        y_copy(nz + t).wait_recv()
        send_x(i, close + yr[nz + t].astype(jnp.float32))
    for i in range(nz):
        own[i] = partial(0, i)
    stores = []
    for h in range(2):
        nf_copies[h].wait_recv()
        picked = pl.ds(h * part, part)
        one = pltpu.make_async_copy(nf.at[picked], nf_hbm.at[picked], store_sem.at[h])
        one.start()
        stores.append(one)
    for k in range(1, n):
        to = (c + k) % n
        copy(ms.at[to], mr.at[n - k], m_sem.at[0], m_sem.at[1], d, to).start()

    def column_sum(i):
        x_copy(i).wait_recv()
        y_copy(i).wait_recv()
        return own[i] + (xr[i].astype(jnp.float32) + yr[i].astype(jnp.float32))

    def z_copy(i):
        to_z = order[i]
        return copy(
            zs.at[i], zr.at[z], z_send.at[i], z_recv.at[z], d, to_z * 4 + xy
        )

    for i in range(nz - 1, 0, -1):
        zs[i] = column_sum(i).astype(jnp.bfloat16)
        z_copy(i).start()
    total = column_sum(0)
    pltpu.make_async_copy(mr.at[pl.ds(1, n - 1)], mr.at[pl.ds(1, n - 1)], m_sem.at[1]).wait()
    mass_total = ms[c]
    for k in range(1, n):
        mass_total = mass_total + mr[k]
    mass_total = to_col(mass_total[0:1])
    for i in range(nz - 1, 0, -1):
        o = order[i]
        copy(zs.at[i], zr.at[o], z_send.at[i], z_recv.at[o], d, o * 4 + xy).wait_recv()
        total = total + zr[o].astype(jnp.float32)
    nc[:, own_cols] = (coarse_prior * coarse[:, own_cols] + total) / (coarse_prior + mass_total)
    last = copy(nc.at[:, own_cols], nc.at[:, own_cols], nc_sem.at[0], nc_sem.at[1], other, c)
    last.start()

    for one in sends:
        one.wait_send()
    for exists, one in maybe_sends:
        @pl.when(exists)
        def _(one=one):
            one.wait_send()

    for i in range(1, nz):
        z_copy(i).wait_send()
    for r in range(4):
        whole = st.at[cols[r], pl.ds(1, n - 1)]
        pltpu.make_async_copy(whole, whole, st_send.at[r]).wait()
    pltpu.make_async_copy(mr.at[pl.ds(1, n - 1)], mr.at[pl.ds(1, n - 1)], m_sem.at[0]).wait()
    for i in range(nz + low):
        x_copy(i).wait_send()
        y_copy(i).wait_send()
    for one in nf_copies:
        one.wait_send()
    for one in stores:
        one.wait()
    last.wait()


def fused_step(n, embeddings, fine_centroids, parents, coarse_centroids):
    nz = n // 4
    low = nz // 2
    rows, width = embeddings.shape
    local = fine_centroids.shape[0]
    coarse_rows = coarse_centroids.shape[0]
    half = width // 2
    bf, f32 = jnp.bfloat16, jnp.float32
    vmem = pl.BlockSpec(memory_space=pltpu.VMEM)
    hbm = pl.BlockSpec(memory_space=pl.ANY)
    dma = pltpu.SemaphoreType.DMA
    V = pltpu.VMEM
    block = (coarse_rows, half)
    return pl.pallas_call(
        functools.partial(step_kernel, n, nz),
        out_shape=(
            jax.ShapeDtypeStruct(fine_centroids.shape, f32),
            jax.ShapeDtypeStruct(coarse_centroids.shape, f32),
        ),
        in_specs=[hbm, hbm, vmem, vmem],
        out_specs=(hbm, vmem),
        scratch_shapes=[
            V((local, width), f32),
            V((local, width), f32),
            V((2, 2, local // 2, half), f32),
            V((n, rows, width), bf),
            V((local, width), bf),
            V((4, local, nz * rows), f32),
            V((4, local, nz * rows), bf),
            V((4, n, 2 * nz, rows), f32),
            V((2, local // 2, half), f32),
            V((2, local // 2, half), f32),
            V((8, local), f32),
            V((8, local), f32),
            V((local, half), bf),
            V((local, half), bf),
            V((nz + low,) + block, bf),
            V((nz + low,) + block, bf),
            V((nz + low,) + block, bf),
            V((nz + low,) + block, bf),
            V((nz,) + block, bf),
            V((nz,) + block, bf),
            V((nz,) + block, f32),
            V((n, 8, coarse_rows), f32),
            V((n, 8, coarse_rows), f32),
            dma((2 * n,)), dma((2 * nz + 2,)), dma((2 * (nz + low),)), dma((2 * (nz + low),)),
            dma((4,)), dma((4,)),
            dma((2,)), dma((2,)), dma((2,)), dma((2,)), dma((2,)),
            dma((nz + low,)), dma((nz + low,)), dma((nz + low,)), dma((nz + low,)),
            dma((nz,)), dma((nz,)), dma((2,)), dma((2,)), dma((2,)), dma((2,)),
        ],
        compiler_params=pltpu.CompilerParams(collective_id=0, has_side_effects=True),
    )(embeddings, fine_centroids, parents.reshape(1, local), coarse_centroids)


def solution(mesh):
    in_specs = (P(("dp", "cent"), None), P("cent", None), P("cent"), P("cent", None))
    out_specs = (P("cent", None), P("cent", None))
    n, cores = mesh.shape["cent"], mesh.shape["dp"]

    def body(embeddings, fine_centroids, parents, coarse_centroids):
        rows, width = embeddings.shape
        fits = (
            cores == 2
            and n % 8 == 0
            and rows == 128
            and width % 256 == 0
            and fine_centroids.shape[0] % 256 == 0
            and coarse_centroids.shape[0] == 128
        )
        if fits:
            return fused_step(n, embeddings, fine_centroids, parents, coarse_centroids)
        return local(embeddings, fine_centroids, parents, coarse_centroids)

    return jax.shard_map(body, mesh=mesh, in_specs=in_specs, out_specs=out_specs, check_vma=False)
```
